128 devices in a mesh: lat: 8 (over y_hi, z), lon: 16 (over y_lo, x, core).
Axes of the slice: x: 4, y: 4 (y_hi: 2, y_lo: 2; y = y_hi * 2 + y_lo), z: 4, core: 2. Of those that a mesh axis runs over, the one named last changes fastest.
Arguments:
- adjoint_final: float32 [8, 16, 256, 4096], P(None, None, 'lat', 'lon'), may hold values from -4 to 4
- courant_lon: float32 [16, 256, 4096], P(None, 'lat', 'lon'), may hold values from -0.25 to 0.25
- courant_lat: float32 [16, 256, 4096], P(None, 'lat', 'lon'), may hold values from -0.25 to 0.25
- diffusivity: float32 [15], replicated, may hold values from 0.02 to 0.24
- scavenging: float32 [8], replicated, may hold values from 0.05 to 1
- lidar_innov: bfloat16 [262144, 128], P(('lat', 'lon')), may hold values from -6 to 6
- lidar_owner: int32 [262144, 1], P(('lat', 'lon')), may hold values from 0 to 127; in each aligned block of 2048 rows (0 to 2047, 2048 to 4095, ...) at most 32 rows name the same one
- lidar_column: int32 [262144], P(('lat', 'lon')), may hold values from 0 to 8191
- radiometer_innov: bfloat16 [262144, 128], P(('lat', 'lon')), may hold values from -6 to 6
- radiometer_owner: int32 [262144, 1], P(('lat', 'lon')), may hold values from 0 to 127; in each aligned block of 2048 rows (0 to 2047, 2048 to 4095, ...) at most 32 rows name the same one
- radiometer_column: int32 [262144], P(('lat', 'lon')), may hold values from 0 to 8191
- obs_count: int32 [128, 2], P(('lat', 'lon')), may hold values from 1024 to 2048, as said below
- lidar_op: bfloat16 [128, 128], replicated, may hold values from -0.5 to 0.5
- radiometer_op: bfloat16 [128, 128], replicated, may hold values from -0.5 to 0.5
Outputs:
- adjoint_initial: float32 [8, 16, 256, 4096], P(None, None, 'lat', 'lon')
The draws below stay inside these ranges and needn't reach their ends.
Inputs may be any that keep to these rules, and one draw needn't show every extreme that they name: `lidar_owner`: at most 32 of one device's 2048 listed rows name one owner, a bound that some block reaches. `radiometer_owner`: at most 32 of one device's 2048 listed rows name one owner, a bound that some block reaches. `obs_count`: rows at or beyond a device's count are unused; for each instrument some device uses all 2048.
All inputs are finite; a program needn't handle non-finite values.
Results may differ from the reference program's by a relative error of at most 0.00081.
Values may be sent and summed in bfloat16 or wider, within the bound.
A program may use at most 64 MiB of HBM per device.

```python
import math
import jax
import jax.numpy as jnp
import numpy as np
from jax import lax

BINS = 8
LEV = 16
CLAT = 32
CLON = 256
OBS_DEV = 2048
STEPS = 3
CAP = 32
NLAT = 256
NLON = 4096
CELLS = 8192
N_LAT = 8
N_LON = 16
DEVICES = 128


def draw_obs_count(key, part):
    first_key, second_key = jax.random.split(key, 2)
    counts = jax.random.randint(first_key, (DEVICES, 2), OBS_DEV // 2, OBS_DEV + 1)
    chosen = jax.random.randint(second_key, (2,), 0, DEVICES)
    counts = counts.at[chosen[0], 0].set(OBS_DEV)
    counts = counts.at[chosen[1], 1].set(OBS_DEV)
    return counts.astype(jnp.int32)


def checker_parity():
    lat_ids = jnp.arange(NLAT, dtype=jnp.int32)[:, None]
    lon_ids = jnp.arange(NLON, dtype=jnp.int32)[None, :]
    return ((lat_ids + lon_ids) % 2 * 2 - 1).astype(jnp.float32)


def draw_adjoint_final(key, part):
    own_key = jax.random.fold_in(key, 301)
    size_key, layer_key = jax.random.split(own_key, 2)
    shape = (BINS, LEV, NLAT, NLON)
    magnitude = jax.random.uniform(size_key, shape, jnp.float32, 2.0, 4.0)
    layer_sign = (jax.random.randint(layer_key, (BINS, LEV, 1, 1), 0, 2) * 2 - 1).astype(jnp.float32)
    return (magnitude * layer_sign * checker_parity()[None, None]).astype(jnp.float32)


def courant_field(key):
    size_key, sign_key = jax.random.split(key, 2)
    shape = (LEV, NLAT, NLON)
    magnitude = jax.random.uniform(size_key, shape, jnp.float32, 0.2, 0.25)
    sign_value = (jax.random.randint(sign_key, shape, 0, 2) * 2 - 1).astype(jnp.float32)
    return (magnitude * sign_value).astype(jnp.float32)


def draw_courant_lon(key, part):
    return courant_field(jax.random.fold_in(key, 302))


def draw_courant_lat(key, part):
    return courant_field(jax.random.fold_in(key, 303))


def with_ends(result, key, low, top_value):
    spot = [jax.random.randint(jax.random.fold_in(key, axis), (), 0, length) for axis, length in enumerate(result.shape)]
    longest = result.shape.index(max(result.shape))
    next_to = spot[:longest] + [(spot[longest] + 1) % result.shape[longest]] + spot[longest + 1:]
    return result.at[tuple(spot)].set(low).at[tuple(next_to)].set(top_value)


def levels(key, dims, shards, low, largest):
    def one(axis_at, shards_of):
        heights = jax.random.uniform(jax.random.fold_in(jax.random.fold_in(key, 6), axis_at), (shards_of,), jnp.float32, low / len(shards), largest / len(shards))
        return jnp.repeat(jnp.exp(heights), dims[axis_at] // shards_of).reshape((-1,) + (1,) * (len(dims) - axis_at - 1))

    level = one(*shards[0])
    for cut in shards[1:]:
        level = level * one(*cut)
    return level


def deal_out(rng, own, number, rows, number_of, top, reach, lean):
    ranking = jax.random.permutation(rng, number_of)
    heavy_load, common = load_shares(number_of, rows * top, reach, lean, True), load_shares(number_of, rows * top, reach, lean, False)
    places = jnp.arange(number_of)

    def named(tallies, rotation):
        used = int((tallies > 0).sum())
        fixed = max(1, used // 4)
        shifted = fixed + (places - fixed + rotation * (used - fixed)) % max(1, number_of - fixed)
        return jnp.zeros((number_of,), jnp.int32).at[ranking[jnp.where(places < fixed, places, shifted)]].set(jnp.asarray(tallies, jnp.int32))

    tallies = jnp.where(number % 4 == 0, named(heavy_load, number // 4), named(common, number - number // 4 - 1))
    mixed = jax.random.permutation(jax.random.fold_in(own, 3), number_of)
    giver, taker = mixed[0:number_of // 2 * 2:2], mixed[1:number_of // 2 * 2:2]
    room = jnp.minimum(tallies[giver] - 1, reach - tallies[taker]) // 2
    room = jnp.where((giver == ranking[0]) | (taker == ranking[0]) | (tallies[taker] == 0), 0, jnp.maximum(room, 0))
    shifted = jax.random.randint(jax.random.fold_in(own, 4), (number_of // 2,), 0, 1 << 20) % (room + 1)
    tallies = tallies.at[giver].add(-shifted).at[taker].add(shifted)
    labels = jnp.searchsorted(jnp.cumsum(tallies), jnp.arange(rows * top), side="right").astype(jnp.int32)
    table = labels.reshape(top, rows).T
    table = table[jax.random.permutation(jax.random.fold_in(own, 1), rows)]
    rotation = jax.random.randint(jax.random.fold_in(own, 2), (rows, 1), 0, top)
    return jnp.take_along_axis(table, (jnp.arange(top)[None, :] + rotation) % top, axis=1)


def load_shares(amount, total, bound, slope, full):
    loads = [(1 << 20) // math.isqrt(standing ** slope) + 1 for standing in range(1, amount + 1)]
    largest = bound if full else min(bound, max(-(-total // amount), total * loads[0] // sum(loads)))
    least = 1 if total - largest >= amount - 1 else 0
    holding, surplus = [largest] + [least] * (amount - 1), total - largest - least * (amount - 1)
    while surplus > 0:
        free = [i for i in range(1, amount) if holding[i] < largest] or [i for i in range(1, amount) if holding[i] < bound]
        whole, budget = sum([loads[i] for i in free]), surplus
        for i in free:
            addition = min(bound - holding[i], max(1, budget * loads[i] // whole), surplus)
            holding[i] = holding[i] + addition
            surplus = surplus - addition
    return np.array(holding)


def normal_values(key, extent, spread, limit, cuts=(), kind=jnp.bfloat16):
    factor_of = levels(key, extent, cuts, -0.22, 0.18) if cuts else 1.0
    values = jax.random.normal(key, extent, jnp.float32) * spread * factor_of
    return jnp.minimum(jnp.maximum(values, -limit), limit).astype(kind)


def setup_inputs(seed: int = 0) -> dict:
    arg_keys = jax.random.split(jax.random.key(seed), 15)
    adjoint_final = draw_adjoint_final(jax.random.fold_in(arg_keys[14], 71), 0)
    courant_lon = draw_courant_lon(jax.random.fold_in(arg_keys[14], 71), 0)
    courant_lat = draw_courant_lat(jax.random.fold_in(arg_keys[14], 71), 0)
    diffusivity = jnp.clip(jnp.exp(jax.random.uniform(arg_keys[3], (LEV - 1,), jnp.float32, math.log(0.02), math.log(0.24))), 0.02, 0.24)
    scavenging = jnp.clip(jnp.exp(jax.random.uniform(arg_keys[4], (BINS,), jnp.float32, math.log(0.05), math.log(1.0))), 0.05, 1.0)
    lidar_innov = normal_values(arg_keys[5], (DEVICES * OBS_DEV, BINS * LEV), 1.0, 6.0, ((0, 128),))
    lidar_owner_keys = jax.random.split(jax.random.fold_in(arg_keys[6], 1), (DEVICES * OBS_DEV) // OBS_DEV)
    lidar_owner_turns = jax.random.permutation(jax.random.fold_in(arg_keys[6], 3), (DEVICES * OBS_DEV) // OBS_DEV)
    lidar_owner = jax.vmap(lambda own, number: deal_out(jax.random.fold_in(arg_keys[6], 2), own, number, OBS_DEV, DEVICES, 1, CAP, 2))(lidar_owner_keys, lidar_owner_turns).reshape((DEVICES * OBS_DEV, 1))
    lidar_column = with_ends(jax.random.randint(arg_keys[7], (DEVICES * OBS_DEV,), 0, CELLS), jax.random.fold_in(arg_keys[7], 1), 0, CELLS - 1).astype(jnp.int32)
    radiometer_innov = normal_values(arg_keys[8], (DEVICES * OBS_DEV, BINS * LEV), 1.0, 6.0, ((0, 128),))
    radiometer_owner_keys = jax.random.split(jax.random.fold_in(arg_keys[9], 1), (DEVICES * OBS_DEV) // OBS_DEV)
    radiometer_owner_turns = jax.random.permutation(jax.random.fold_in(arg_keys[9], 3), (DEVICES * OBS_DEV) // OBS_DEV)
    radiometer_owner = jax.vmap(lambda own, number: deal_out(jax.random.fold_in(arg_keys[9], 2), own, number, OBS_DEV, DEVICES, 1, CAP, 1))(radiometer_owner_keys, radiometer_owner_turns).reshape((DEVICES * OBS_DEV, 1))
    radiometer_column = with_ends(jax.random.randint(arg_keys[10], (DEVICES * OBS_DEV,), 0, CELLS), jax.random.fold_in(arg_keys[10], 1), 0, CELLS - 1).astype(jnp.int32)
    obs_count = draw_obs_count(jax.random.fold_in(arg_keys[14], 71), 0)
    lidar_op = normal_values(arg_keys[12], (BINS * LEV, BINS * LEV), (BINS * LEV) ** -0.5, 0.5)
    radiometer_op = normal_values(arg_keys[13], (BINS * LEV, BINS * LEV), (BINS * LEV) ** -0.5, 0.5)
    return dict(adjoint_final=adjoint_final, courant_lon=courant_lon, courant_lat=courant_lat, diffusivity=diffusivity, scavenging=scavenging, lidar_innov=lidar_innov, lidar_owner=lidar_owner, lidar_column=lidar_column, radiometer_innov=radiometer_innov, radiometer_owner=radiometer_owner, radiometer_column=radiometer_column, obs_count=obs_count, lidar_op=lidar_op, radiometer_op=radiometer_op)


def vertical_mix(adjoint, decay_factor, diffusivity):
    scaled = adjoint * decay_factor[:, None, None, None]
    differ = (scaled[:, 1:] - scaled[:, :-1]) * diffusivity[None, :, None, None]
    border = jnp.zeros_like(scaled[:, :1])
    fluxes = jnp.concatenate([border, differ, border], axis=1)
    return scaled + fluxes[:, 1:] - fluxes[:, :-1]


def advect_back(adjoint, east_side, west_side, north_side, south_side, lon_here, lon_next, lat_here, lat_next):
    return (adjoint + lon_next[None] * (east_side - adjoint) + lon_here[None] * (adjoint - west_side)
            + lat_next[None] * (north_side - adjoint) + lat_here[None] * (adjoint - south_side))


def reference(adjoint_final, courant_lon, courant_lat, diffusivity, scavenging, lidar_innov, lidar_owner,
              lidar_column, radiometer_innov, radiometer_owner, radiometer_column, obs_count, lidar_op,
              radiometer_op):
    devices = N_LAT * N_LON
    row_width = BINS * LEV
    total_lat = CLAT * N_LAT
    total_lon = CLON * N_LON

    def place(innovation, owners, column, kind, obs_operator):
        values = jnp.dot(innovation, obs_operator, preferred_element_type=jnp.float32).astype(jnp.bfloat16)
        row_index = jnp.arange(devices * OBS_DEV, dtype=jnp.int32)
        source = row_index // OBS_DEV
        local_index = row_index % OBS_DEV
        usable = local_index < obs_count[source, kind]
        target = owners[:, 0]
        global_lat = (target // N_LON) * CLAT + column // CLON
        global_lon = (target % N_LON) * CLON + column % CLON
        flat_cell = jnp.where(usable, global_lat * total_lon + global_lon, total_lat * total_lon)
        return values, flat_cell.astype(jnp.int32)

    lidar_values, lidar_cells = place(lidar_innov, lidar_owner, lidar_column, 0, lidar_op)
    radio_values, radio_cells = place(radiometer_innov, radiometer_owner, radiometer_column, 1, radiometer_op)
    all_values = lax.optimization_barrier(jnp.concatenate([lidar_values, radio_values], axis=0))
    all_values = all_values.astype(jnp.float32)
    all_cells = jnp.concatenate([lidar_cells, radio_cells], axis=0)
    flat_adjoint = adjoint_final.reshape(row_width, total_lat * total_lon)
    flat_adjoint = flat_adjoint.at[:, all_cells].add(all_values.T, mode="drop")
    adjoint = flat_adjoint.reshape(BINS, LEV, total_lat, total_lon)

    decay_factor = jnp.exp(-scavenging)
    lon_here = jnp.minimum(courant_lon, 0.0)
    lon_next = jnp.maximum(jnp.roll(courant_lon, -1, axis=2), 0.0)
    row_ids = jnp.arange(total_lat, dtype=jnp.int32)
    lat_face = jnp.where(row_ids[None, :, None] == 0, 0.0, courant_lat)
    lat_here = jnp.minimum(lat_face, 0.0)
    lat_next = jnp.maximum(jnp.concatenate([lat_face[:, 1:], jnp.zeros_like(lat_face[:, :1])], axis=1), 0.0)

    def evolve(pair):
        bin_adjoint = pair[0][None]
        bin_decay = jnp.reshape(pair[1], (1,))
        for step_index in range(STEPS):
            mixed_adjoint = vertical_mix(bin_adjoint, bin_decay, diffusivity)
            east_side = jnp.roll(mixed_adjoint, -1, axis=3)
            west_side = jnp.roll(mixed_adjoint, 1, axis=3)
            border = jnp.zeros_like(mixed_adjoint[:, :, :1])
            north_side = jnp.concatenate([mixed_adjoint[:, :, 1:], border], axis=2)
            south_side = jnp.concatenate([border, mixed_adjoint[:, :, :-1]], axis=2)
            bin_adjoint = advect_back(mixed_adjoint, east_side, west_side, north_side, south_side,
                                      lon_here, lon_next, lat_here, lat_next)
        return bin_adjoint[0]

    return lax.map(evolve, (adjoint, decay_factor))
```

```python
import functools

import jax
import jax.numpy as jnp
from jax import lax
from jax.experimental import pallas as pl
from jax.experimental.pallas import tpu as pltpu
from jax.sharding import PartitionSpec as P

MESH = pl.DeviceIdType.MESH
STEPS = 3
LANES = 128


def lane_roll(x, amount):
    amount = amount % x.shape[1]
    return x if amount == 0 else pltpu.roll(x, amount, axis=1)


def transport_kernel(
    lat_count,
    lon_count,
    diff_ref,
    scav_ref,
    adj_ref,
    clon_ref,
    clat_ref,
    out_ref,
    mixed_ref,
    c0_ref,
    ce_ref,
    cw_ref,
    cn_ref,
    cs_ref,
    srow,
    rrow,
    scol,
    rcol,
    fsrow,
    frrow,
    fscol,
    frcol,
    row_send,
    row_recv,
    col_send,
    col_recv,
    face_send,
    face_recv,
):
    bins, levels, rows, cols = adj_ref.shape
    lat = lax.axis_index("lat")
    lon = lax.axis_index("lon")
    north = {"lat": lax.rem(lat + 1, lat_count)}
    south = {"lat": lax.rem(lat + lat_count - 1, lat_count)}
    east = {"lon": lax.rem(lon + 1, lon_count)}
    west = {"lon": lax.rem(lon + lon_count - 1, lon_count)}

    barrier = pltpu.get_barrier_semaphore()
    for there in (north, south, east, west):
        pl.semaphore_signal(barrier, inc=1, device_id=there, device_id_type=MESH)
    pl.semaphore_wait(barrier, 4)

    lane = lax.broadcasted_iota(jnp.int32, (rows, LANES), 1)
    is_first = lane == 0
    is_last = lane == LANES - 1
    sub = lax.broadcasted_iota(jnp.int32, (8, cols), 0)
    top = sub == 7
    bottom = sub == 0

    def remote(src, dst, send, recv, there):
        return pltpu.make_async_remote_copy(
            src_ref=src, dst_ref=dst, send_sem=send, recv_sem=recv, device_id=there, device_id_type=MESH
        )

    def face_copies():
        return (
            remote(fsrow, frrow, face_send.at[0], face_recv.at[0], south),
            remote(fscol, frcol, face_send.at[1], face_recv.at[1], west),
        )

    def halo_copies(t):
        return (
            remote(srow.at[0, t], rrow.at[0, t], row_send.at[0, t], row_recv.at[0, t], south),
            remote(srow.at[1, t], rrow.at[1, t], row_send.at[1, t], row_recv.at[1, t], north),
            remote(scol.at[0, t], rcol.at[0, t], col_send.at[0, t], col_recv.at[0, t], west),
            remote(scol.at[1, t], rcol.at[1, t], col_send.at[1, t], col_recv.at[1, t], east),
        )

    packed = jnp.zeros((rows, LANES), jnp.float32)
    for l in range(levels):
        fsrow[l : l + 1, :] = clat_ref[l, 0:1, :]
        packed = jnp.where(lane == l, lane_roll(clon_ref[l, :, 0:LANES], l), packed)
    fscol[...] = packed
    for copy in face_copies():
        copy.start()

    def emit(value, l, b, t, packs):
        mixed_ref[b, l] = value
        srow[0, t, l : l + 1, :] = value[0:1, :]
        srow[1, t, l : l + 1, :] = value[rows - 1 : rows, :]
        west_pack, east_pack = packs
        west_pack = jnp.where(lane == l, lane_roll(value[:, 0:LANES], l), west_pack)
        east_pack = jnp.where(lane == l, lane_roll(value[:, LANES:], l + 1), east_pack)
        return west_pack, east_pack

    def mix_and_send(plane, b, t):
        zero = jnp.zeros((rows, LANES), jnp.float32)
        packs = (zero, zero)
        here = plane(0)
        flux_low = None
        for l in range(levels):
            value = here
            if l + 1 < levels:
                above = plane(l + 1)
                flux_high = (above - here) * diff_ref[l]
                value = value + flux_high
            if flux_low is not None:
                value = value - flux_low
            packs = emit(value, l, b, t, packs)
            if l + 1 < levels:
                here, flux_low = above, flux_high
        scol[0, t] = packs[0]
        scol[1, t] = packs[1]
        for copy in halo_copies(t):
            copy.start()

    @pl.loop(0, bins)
    def _(b):
        factor = jnp.exp(jnp.full((8, LANES), -3.0 * scav_ref[b], jnp.float32))
        factor = jnp.concatenate([factor] * (rows // 8), axis=0)
        factor = jnp.concatenate([factor] * (cols // LANES), axis=1)
        mix_and_send(lambda l: adj_ref[b, l] * factor, b, b)

    for copy in face_copies():
        copy.wait()
    row_index = lax.broadcasted_iota(jnp.int32, (rows, cols), 0)
    first_band = (lat == 0).astype(jnp.int32)
    last_band = (lat == lat_count - 1).astype(jnp.int32)
    south_open = jnp.where(row_index + rows * (1 - first_band) == 0, 0.0, 1.0)
    north_open = jnp.where(row_index + rows * (1 - last_band) == rows - 1, 0.0, 1.0)
    for l in range(levels):
        face = clon_ref[l]
        left, right = lane_roll(face[:, 0:LANES], LANES - 1), lane_roll(face[:, LANES:], LANES - 1)
        outer = lane_roll(frcol[...], LANES - 1 - l)
        beyond = jnp.concatenate([jnp.where(is_last, right, left), jnp.where(is_last, outer, right)], axis=1)
        lon_next = jnp.maximum(beyond, 0.0)
        lon_here = jnp.minimum(face, 0.0)
        face = clat_ref[l]
        up = pltpu.roll(face, rows - 1, axis=0)
        edge = jnp.where(top, jnp.broadcast_to(frrow[l : l + 1, :], (8, cols)), up[rows - 8 :])
        up = jnp.concatenate([up[: rows - 8], edge], axis=0)
        lat_next = jnp.maximum(up, 0.0) * north_open
        lat_here = jnp.minimum(face, 0.0) * south_open
        ce_ref[l] = lon_next
        cw_ref[l] = -lon_here
        cn_ref[l] = lat_next
        cs_ref[l] = -lat_here
        c0_ref[l] = 1.0 - lon_next + lon_here - lat_next + lat_here

    def advected(b, t):
        def plane(l):
            m = mixed_ref[b, l]
            m0, m1 = m[:, 0:LANES], m[:, LANES:]
            r0, r1 = lane_roll(m0, 1), lane_roll(m1, 1)
            q0, q1 = lane_roll(m0, LANES - 1), lane_roll(m1, LANES - 1)
            west_halo = lane_roll(rcol[1, t], LANES - l)
            east_halo = lane_roll(rcol[0, t], LANES - 1 - l)
            w = jnp.concatenate([jnp.where(is_first, west_halo, r0), jnp.where(is_first, r0, r1)], axis=1)
            e = jnp.concatenate([jnp.where(is_last, q1, q0), jnp.where(is_last, east_halo, q1)], axis=1)
            n = pltpu.roll(m, rows - 1, axis=0)
            s = pltpu.roll(m, 1, axis=0)
            north_halo = jnp.broadcast_to(rrow[0, t, l : l + 1, :], (8, cols))
            south_halo = jnp.broadcast_to(rrow[1, t, l : l + 1, :], (8, cols))
            n = jnp.concatenate([n[: rows - 8], jnp.where(top, north_halo, n[rows - 8 :])], axis=0)
            s = jnp.concatenate([jnp.where(bottom, south_halo, s[:8]), s[8:]], axis=0)
            return c0_ref[l] * m + ce_ref[l] * e + cw_ref[l] * w + cn_ref[l] * n + cs_ref[l] * s

        return plane

    def arrive(t):
        for copy in halo_copies(t):
            copy.wait_recv()

    @pl.loop(0, (STEPS - 1) * bins)
    def _(t):
        arrive(t)
        b = lax.rem(t, bins)
        mix_and_send(advected(b, t), b, t + bins)

    @pl.loop((STEPS - 1) * bins, STEPS * bins)
    def _(t):
        arrive(t)
        b = lax.rem(t, bins)
        plane = advected(b, t)
        for l in range(levels):
            out_ref[b, l] = plane(l)

    @pl.loop(0, STEPS * bins)
    def _(t):
        for copy in halo_copies(t):
            copy.wait_send()


def transport(adjoint, courant_lon, courant_lat, diffusivity, scavenging):
    bins, levels, rows, cols = adjoint.shape
    turns = STEPS * bins
    vmem = pl.BlockSpec(memory_space=pltpu.VMEM)
    smem = pl.BlockSpec(memory_space=pltpu.SMEM)
    f32 = jnp.float32
    coef = pltpu.VMEM((levels, rows, cols), f32)
    return pl.pallas_call(
        functools.partial(transport_kernel, lax.axis_size("lat"), lax.axis_size("lon")),
        out_shape=jax.ShapeDtypeStruct(adjoint.shape, f32),
        in_specs=[smem, smem, vmem, vmem, vmem],
        out_specs=vmem,
        scratch_shapes=[
            pltpu.VMEM(adjoint.shape, f32),
            coef,
            coef,
            coef,
            coef,
            coef,
            pltpu.VMEM((2, turns, levels, cols), f32),
            pltpu.VMEM((2, turns, levels, cols), f32),
            pltpu.VMEM((2, turns, rows, LANES), f32),
            pltpu.VMEM((2, turns, rows, LANES), f32),
            pltpu.VMEM((levels, cols), f32),
            pltpu.VMEM((levels, cols), f32),
            pltpu.VMEM((rows, LANES), f32),
            pltpu.VMEM((rows, LANES), f32),
            pltpu.SemaphoreType.DMA((2, turns)),
            pltpu.SemaphoreType.DMA((2, turns)),
            pltpu.SemaphoreType.DMA((2, turns)),
            pltpu.SemaphoreType.DMA((2, turns)),
            pltpu.SemaphoreType.DMA((2,)),
            pltpu.SemaphoreType.DMA((2,)),
        ],
        compiler_params=pltpu.CompilerParams(collective_id=0, has_side_effects=True, vmem_limit_bytes=60 << 20),
    )(diffusivity, scavenging, adjoint, courant_lon, courant_lat)


def per_device(
    adjoint_final,
    courant_lon,
    courant_lat,
    diffusivity,
    scavenging,
    lidar_innov,
    lidar_owner,
    lidar_column,
    radiometer_innov,
    radiometer_owner,
    radiometer_column,
    obs_count,
    lidar_op,
    radiometer_op,
):
    lat_count = lax.axis_size("lat")
    lon_count = lax.axis_size("lon")
    devices = lat_count * lon_count
    bin_count, levels, band_rows, block_cols = adjoint_final.shape
    row_width = bin_count * levels
    cell_count = band_rows * block_cols
    obs_rows = lidar_innov.shape[0]
    capacity = max(2, 2 * obs_rows // devices)
    slots = 2 * capacity

    def bucket(innovation, owners, column, used_count, obs_operator, offset):
        values = jnp.dot(innovation, obs_operator, preferred_element_type=jnp.float32).astype(
            jnp.bfloat16
        )
        usable = jnp.arange(obs_rows, dtype=jnp.int32) < used_count
        target = owners[:, 0]
        member = (target[:, None] == jnp.arange(devices, dtype=jnp.int32)[None, :]) & usable[
            :, None
        ]
        member = member.astype(jnp.int32)
        before = jnp.cumsum(member, axis=0) - member
        slot_index = jnp.sum(before * member, axis=1)
        position = jnp.where(usable, target * slots + offset + slot_index, devices * slots)
        return (values, column, position)

    lidar_values, lidar_cols, lidar_pos = bucket(
        lidar_innov, lidar_owner, lidar_column, obs_count[0, 0], lidar_op, 0
    )
    radio_values, radio_cols, radio_pos = bucket(
        radiometer_innov,
        radiometer_owner,
        radiometer_column,
        obs_count[0, 1],
        radiometer_op,
        capacity,
    )
    all_values = jnp.concatenate([lidar_values, radio_values], axis=0)
    all_cols = jnp.concatenate([lidar_cols, radio_cols], axis=0)
    all_pos = jnp.concatenate([lidar_pos, radio_pos], axis=0)
    send_rows = (
        jnp.zeros((devices * slots, row_width), jnp.bfloat16)
        .at[all_pos]
        .set(all_values, mode="drop")
    )
    send_cols = (
        jnp.full((devices * slots,), cell_count, jnp.int32).at[all_pos].set(all_cols, mode="drop")
    )
    got_rows, got_cols = (
        lax.all_to_all(send_rows, ("lat", "lon"), split_axis=0, concat_axis=0, tiled=True),
        lax.all_to_all(send_cols, ("lat", "lon"), split_axis=0, concat_axis=0, tiled=True),
    )
    forcing = jnp.zeros((row_width, cell_count), jnp.float32)
    forcing = forcing.at[:, got_cols].add(got_rows.astype(jnp.float32).T, mode="drop")
    adjoint = (adjoint_final.reshape(row_width, cell_count) + forcing).reshape(
        bin_count, levels, band_rows, block_cols
    )
    return transport(adjoint, courant_lon, courant_lat, diffusivity, scavenging)


def solution(mesh):
    return jax.shard_map(
        per_device,
        mesh=mesh,
        in_specs=(
            P(None, None, "lat", "lon"),
            P(None, "lat", "lon"),
            P(None, "lat", "lon"),
            P(),
            P(),
            P(("lat", "lon"), None),
            P(("lat", "lon"), None),
            P(("lat", "lon")),
            P(("lat", "lon"), None),
            P(("lat", "lon"), None),
            P(("lat", "lon")),
            P(("lat", "lon"), None),
            P(),
            P(),
        ),
        out_specs=P(None, None, "lat", "lon"),
        check_vma=False,
    )
```

```python
import functools

import jax
import jax.numpy as jnp
from jax import lax
from jax.experimental import pallas as pl
from jax.experimental.pallas import tpu as pltpu
from jax.sharding import PartitionSpec as P

MESH = pl.DeviceIdType.MESH
STEPS = 3
LANES = 128


def lane_roll(x, amount):
    amount = amount % x.shape[1]
    return x if amount == 0 else pltpu.roll(x, amount, axis=1)


def transport_kernel(
    lat_count,
    lon_count,
    diff_ref,
    scav_ref,
    adj_ref,
    clon_ref,
    clat_ref,
    out_ref,
    mixed_ref,
    c0_ref,
    ce_ref,
    cw_ref,
    cn_ref,
    cs_ref,
    srow,
    rrow,
    scol,
    rcol,
    fsrow,
    frrow,
    fscol,
    frcol,
    row_send,
    row_recv,
    col_send,
    col_recv,
    face_send,
    face_recv,
):
    bins, levels, rows, cols = adj_ref.shape
    lat = lax.axis_index("lat")
    lon = lax.axis_index("lon")
    north = {"lat": lax.rem(lat + 1, lat_count)}
    south = {"lat": lax.rem(lat + lat_count - 1, lat_count)}
    east = {"lon": lax.rem(lon + 1, lon_count)}
    west = {"lon": lax.rem(lon + lon_count - 1, lon_count)}

    barrier = pltpu.get_barrier_semaphore()
    for there in (north, south, east, west):
        pl.semaphore_signal(barrier, inc=1, device_id=there, device_id_type=MESH)
    pl.semaphore_wait(barrier, 4)

    lane = lax.broadcasted_iota(jnp.int32, (rows, LANES), 1)
    is_first = lane == 0
    is_last = lane == LANES - 1
    sub = lax.broadcasted_iota(jnp.int32, (8, cols), 0)
    top = sub == 7
    bottom = sub == 0

    def remote(src, dst, send, recv, there):
        return pltpu.make_async_remote_copy(
            src_ref=src, dst_ref=dst, send_sem=send, recv_sem=recv, device_id=there, device_id_type=MESH
        )

    def face_copies():
        return (
            remote(fsrow, frrow, face_send.at[0], face_recv.at[0], south),
            remote(fscol, frcol, face_send.at[1], face_recv.at[1], west),
        )

    def halo_copies(t):
        return (
            remote(srow.at[0, t], rrow.at[0, t], row_send.at[0, t], row_recv.at[0, t], south),
            remote(srow.at[1, t], rrow.at[1, t], row_send.at[1, t], row_recv.at[1, t], north),
            remote(scol.at[0, t], rcol.at[0, t], col_send.at[0, t], col_recv.at[0, t], west),
            remote(scol.at[1, t], rcol.at[1, t], col_send.at[1, t], col_recv.at[1, t], east),
        )

    packed = jnp.zeros((rows, LANES), jnp.float32)
    for l in range(levels):
        fsrow[l : l + 1, :] = clat_ref[l, 0:1, :]
        packed = jnp.where(lane == l, lane_roll(clon_ref[l, :, 0:LANES], l), packed)
    fscol[...] = packed
    for copy in face_copies():
        copy.start()

    def emit(value, l, b, t, packs):
        mixed_ref[b, l] = value
        srow[0, t, l : l + 1, :] = value[0:1, :]
        srow[1, t, l : l + 1, :] = value[rows - 1 : rows, :]
        west_pack, east_pack = packs
        west_pack = jnp.where(lane == l, lane_roll(value[:, 0:LANES], l), west_pack)
        east_pack = jnp.where(lane == l, lane_roll(value[:, LANES:], l + 1), east_pack)
        return west_pack, east_pack

    def mix_and_send(plane, b, t):
        zero = jnp.zeros((rows, LANES), jnp.float32)
        packs = (zero, zero)
        here = plane(0)
        flux_low = None
        for l in range(levels):
            value = here
            if l + 1 < levels:
                above = plane(l + 1)
                flux_high = (above - here) * diff_ref[l]
                value = value + flux_high
            if flux_low is not None:
                value = value - flux_low
            packs = emit(value, l, b, t, packs)
            if l + 1 < levels:
                here, flux_low = above, flux_high
        scol[0, t] = packs[0]
        scol[1, t] = packs[1]
        for copy in halo_copies(t):
            copy.start()

    @pl.loop(0, bins)
    def _(b):
        factor = jnp.exp(jnp.full((8, LANES), -3.0 * scav_ref[b], jnp.float32))
        factor = jnp.concatenate([factor] * (rows // 8), axis=0)
        factor = jnp.concatenate([factor] * (cols // LANES), axis=1)
        mix_and_send(lambda l: adj_ref[b, l] * factor, b, b)

    for copy in face_copies():
        copy.wait()
    row_index = lax.broadcasted_iota(jnp.int32, (rows, cols), 0)
    first_band = (lat == 0).astype(jnp.int32)
    last_band = (lat == lat_count - 1).astype(jnp.int32)
    south_open = jnp.where(row_index + rows * (1 - first_band) == 0, 0.0, 1.0)
    north_open = jnp.where(row_index + rows * (1 - last_band) == rows - 1, 0.0, 1.0)
    for l in range(levels):
        face = clon_ref[l]
        left, right = lane_roll(face[:, 0:LANES], LANES - 1), lane_roll(face[:, LANES:], LANES - 1)
        outer = lane_roll(frcol[...], LANES - 1 - l)
        beyond = jnp.concatenate([jnp.where(is_last, right, left), jnp.where(is_last, outer, right)], axis=1)
        lon_next = jnp.maximum(beyond, 0.0)
        lon_here = jnp.minimum(face, 0.0)
        face = clat_ref[l]
        up = pltpu.roll(face, rows - 1, axis=0)
        edge = jnp.where(top, jnp.broadcast_to(frrow[l : l + 1, :], (8, cols)), up[rows - 8 :])
        up = jnp.concatenate([up[: rows - 8], edge], axis=0)
        lat_next = jnp.maximum(up, 0.0) * north_open
        lat_here = jnp.minimum(face, 0.0) * south_open
        ce_ref[l] = lon_next
        cw_ref[l] = -lon_here
        cn_ref[l] = lat_next
        cs_ref[l] = -lat_here
        c0_ref[l] = 1.0 - lon_next + lon_here - lat_next + lat_here

    def advected(b, t):
        def plane(l):
            m = mixed_ref[b, l]
            m0, m1 = m[:, 0:LANES], m[:, LANES:]
            r0, r1 = lane_roll(m0, 1), lane_roll(m1, 1)
            q0, q1 = lane_roll(m0, LANES - 1), lane_roll(m1, LANES - 1)
            west_halo = lane_roll(rcol[1, t], LANES - l)
            east_halo = lane_roll(rcol[0, t], LANES - 1 - l)
            w = jnp.concatenate([jnp.where(is_first, west_halo, r0), jnp.where(is_first, r0, r1)], axis=1)
            e = jnp.concatenate([jnp.where(is_last, q1, q0), jnp.where(is_last, east_halo, q1)], axis=1)
            n = pltpu.roll(m, rows - 1, axis=0)
            s = pltpu.roll(m, 1, axis=0)
            north_halo = jnp.broadcast_to(rrow[0, t, l : l + 1, :], (8, cols))
            south_halo = jnp.broadcast_to(rrow[1, t, l : l + 1, :], (8, cols))
            n = jnp.concatenate([n[: rows - 8], jnp.where(top, north_halo, n[rows - 8 :])], axis=0)
            s = jnp.concatenate([jnp.where(bottom, south_halo, s[:8]), s[8:]], axis=0)
            return c0_ref[l] * m + ce_ref[l] * e + cw_ref[l] * w + cn_ref[l] * n + cs_ref[l] * s

        return plane

    def arrive(t):
        for copy in halo_copies(t):
            copy.wait_recv()

    @pl.loop(0, (STEPS - 1) * bins)
    def _(t):
        arrive(t)
        b = lax.rem(t, bins)
        mix_and_send(advected(b, t), b, t + bins)

    @pl.loop((STEPS - 1) * bins, STEPS * bins)
    def _(t):
        arrive(t)
        b = lax.rem(t, bins)
        plane = advected(b, t)
        for l in range(levels):
            out_ref[b, l] = plane(l)

    @pl.loop(0, STEPS * bins)
    def _(t):
        for copy in halo_copies(t):
            copy.wait_send()


def transport(adjoint, courant_lon, courant_lat, diffusivity, scavenging):
    bins, levels, rows, cols = adjoint.shape
    turns = STEPS * bins
    vmem = pl.BlockSpec(memory_space=pltpu.VMEM)
    smem = pl.BlockSpec(memory_space=pltpu.SMEM)
    f32 = jnp.float32
    coef = pltpu.VMEM((levels, rows, cols), f32)
    return pl.pallas_call(
        functools.partial(transport_kernel, lax.axis_size("lat"), lax.axis_size("lon")),
        out_shape=jax.ShapeDtypeStruct(adjoint.shape, f32),
        in_specs=[smem, smem, vmem, vmem, vmem],
        out_specs=vmem,
        scratch_shapes=[
            pltpu.VMEM(adjoint.shape, f32),
            coef,
            coef,
            coef,
            coef,
            coef,
            pltpu.VMEM((2, turns, levels, cols), f32),
            pltpu.VMEM((2, turns, levels, cols), f32),
            pltpu.VMEM((2, turns, rows, LANES), f32),
            pltpu.VMEM((2, turns, rows, LANES), f32),
            pltpu.VMEM((levels, cols), f32),
            pltpu.VMEM((levels, cols), f32),
            pltpu.VMEM((rows, LANES), f32),
            pltpu.VMEM((rows, LANES), f32),
            pltpu.SemaphoreType.DMA((2, turns)),
            pltpu.SemaphoreType.DMA((2, turns)),
            pltpu.SemaphoreType.DMA((2, turns)),
            pltpu.SemaphoreType.DMA((2, turns)),
            pltpu.SemaphoreType.DMA((2,)),
            pltpu.SemaphoreType.DMA((2,)),
        ],
        compiler_params=pltpu.CompilerParams(collective_id=0, has_side_effects=True, vmem_limit_bytes=60 << 20),
    )(diffusivity, scavenging, adjoint, courant_lon, courant_lat)


SLOTS = 32
PEERS = 8


def exchange_kernel(
    lat_split,
    count_ref,
    adj_ref,
    lidar_ref,
    radio_ref,
    lidar_op_ref,
    radio_op_ref,
    lidar_owner_ref,
    radio_owner_ref,
    lidar_col_ref,
    radio_col_ref,
    out_ref,
    table_ref,
    pos_ref,
    pick_ref,
    sent,
    got,
    sent_meta,
    got_meta,
    spread_ref,
    sum_ref,
    send_sem,
    recv_sem,
    meta_send_sem,
    meta_recv_sem,
):
    f32, bf16 = jnp.float32, jnp.bfloat16
    lat_high, lat_low, lon_high, lon_low = lat_split
    peers, _, width = sent.shape
    obs_rows = lidar_ref.shape[0]
    _, rows, cols = adj_ref.shape
    lat = lax.axis_index("lat")
    lon = lax.axis_index("lon")
    lat_count, lon_count = lat_high * lat_low, lon_high * lon_low * 2

    def moved(k, sign):
        core = k % 2
        x = k // 2 % lon_low
        ylow = k // (2 * lon_low) % lon_high
        z = k // (2 * lon_low * lon_high) % lat_low
        yhigh = k // (2 * lon_low * lon_high * lat_low)

        def turn(at, by, size):
            return lax.rem(at + size + sign * by, size)

        to_lat = turn(lat // lat_low, yhigh, lat_high) * lat_low + turn(lat % lat_low, z, lat_low)
        place = lon // 2
        to_lon = turn(place // lon_low, ylow, lon_high) * lon_low + turn(place % lon_low, x, lon_low)
        return to_lat, to_lon * 2 + turn(lon % 2, core, 2)

    barrier = pltpu.get_barrier_semaphore()

    @pl.loop(1, peers)
    def _(k):
        to_lat, to_lon = moved(k, 1)
        pl.semaphore_signal(barrier, inc=1, device_id={"lat": to_lat, "lon": to_lon}, device_id_type=MESH)

    block = 256
    earlier = (
        lax.broadcasted_iota(jnp.int32, (block, block), 0) < lax.broadcasted_iota(jnp.int32, (block, block), 1)
    ).astype(f32).astype(bf16)
    eye = (
        lax.broadcasted_iota(jnp.int32, (width, width), 0) == lax.broadcasted_iota(jnp.int32, (width, width), 1)
    ).astype(f32).astype(bf16)
    nt = (((1,), (1,)), ((), ()))

    def prepare(kind, values_ref, op_ref, owner_ref, col_ref):
        device = lax.broadcasted_iota(jnp.int32, (peers, block), 0)
        sub = lax.broadcasted_iota(jnp.int32, (width, block), 0)
        running = jnp.zeros((peers, 1), f32)
        for n in range(obs_rows // block):
            span = slice(n * block, (n + 1) * block)
            forces = jnp.dot(values_ref[span, :], op_ref[...], preferred_element_type=f32)
            table_ref[kind, span, 0:width] = forces.astype(bf16)
            column = col_ref[:, span]
            meta = jnp.where(sub == 0, column % cols, jnp.where(sub == 1, column // cols, 0)).astype(f32)
            table_ref[kind, span, width:] = meta.T.astype(bf16)
            index = n * block + lax.broadcasted_iota(jnp.int32, (1, block), 1)
            used = index < count_ref[0, kind]
            target = jnp.where(used, owner_ref[:, span], -1)
            member = (target == device).astype(f32)
            before = jnp.dot(member.astype(bf16), earlier, preferred_element_type=f32) + running
            slot = jnp.sum(before * member, axis=0, keepdims=True)
            running = running + jnp.sum(member, axis=1, keepdims=True)
            pos_ref[kind, :, span] = jnp.where(used, target * SLOTS + slot.astype(jnp.int32), -1)

    prepare(0, lidar_ref, lidar_op_ref, lidar_owner_ref, lidar_col_ref)
    prepare(1, radio_ref, radio_op_ref, radio_owner_ref, radio_col_ref)
    pl.semaphore_wait(barrier, peers - 1)

    def copies(k):
        to_lat, to_lon = moved(k, 1)
        there = {"lat": to_lat, "lon": to_lon}
        return (
            pltpu.make_async_remote_copy(
                src_ref=sent.at[k], dst_ref=got.at[k], send_sem=send_sem.at[k], recv_sem=recv_sem.at[k],
                device_id=there, device_id_type=MESH,
            ),
            pltpu.make_async_remote_copy(
                src_ref=sent_meta.at[k], dst_ref=got_meta.at[k], send_sem=meta_send_sem.at[k],
                recv_sem=meta_recv_sem.at[k], device_id=there, device_id_type=MESH,
            ),
        )

    def own_copies():
        return (
            pltpu.make_async_copy(sent.at[0], got.at[0], recv_sem.at[0]),
            pltpu.make_async_copy(sent_meta.at[0], got_meta.at[0], meta_recv_sem.at[0]),
        )

    slot_index = lax.broadcasted_iota(jnp.int32, (SLOTS, obs_rows), 0)
    lane = lax.broadcasted_iota(jnp.int32, (1, LANES), 1)

    @pl.loop(0, peers // PEERS)
    def _(g):
        metas = []
        for kind in range(2):
            for p in range(PEERS):
                to_lat, to_lon = moved(g * PEERS + p, 1)
                local = pos_ref[kind] - (to_lat * lon_count + to_lon) * SLOTS
                pick_ref[p * SLOTS : (p + 1) * SLOTS, :] = (slot_index == local).astype(f32).astype(bf16)
            placed = jnp.dot(pick_ref[...], table_ref[kind], preferred_element_type=f32).astype(bf16)
            for p in range(PEERS):
                sent[g * PEERS + p, kind * SLOTS : (kind + 1) * SLOTS, :] = placed[p * SLOTS : (p + 1) * SLOTS, 0:width]
            metas.append(lax.dot_general(eye[0:16], placed[:, width:], nt, preferred_element_type=f32))
        for p in range(PEERS):
            def piece(kind, what, at):
                half = metas[kind][what : what + 1, p // 4 * LANES : (p // 4 + 1) * LANES]
                return lane_roll(half, at * SLOTS - p % 4 * SLOTS)

            low = jnp.where(lane < SLOTS, piece(0, 0, 0), piece(1, 0, 1))
            high = jnp.where(lane < 3 * SLOTS, piece(0, 1, 2), piece(1, 1, 3))
            sent_meta[g * PEERS + p] = jnp.where(lane < 2 * SLOTS, low, high)
        for p in range(PEERS):
            @pl.when(g * PEERS + p > 0)
            def _():
                for copy in copies(g * PEERS + p):
                    copy.start()

        @pl.when(g == 0)
        def _():
            for copy in own_copies():
                copy.start()

    @pl.loop(0, rows)
    def _(r):
        sum_ref[r] = jnp.zeros((2, width, LANES), f32)

    depth = PEERS * 2 * SLOTS
    col_index = lax.broadcasted_iota(jnp.int32, (cols, depth), 0).astype(f32)

    @pl.loop(0, peers // PEERS)
    def _(g):
        for p in range(PEERS):
            @pl.when(g * PEERS + p > 0)
            def _():
                for copy in copies(g * PEERS + p):
                    copy.wait_recv()

        @pl.when(g == 0)
        def _():
            for copy in own_copies():
                copy.wait()

        c_parts, r_parts = [], []
        for p in range(0, PEERS, 2):
            one, two = got_meta[g * PEERS + p], got_meta[g * PEERS + p + 1]
            c_parts.append(jnp.where(lane < 2 * SLOTS, one, lane_roll(two, 2 * SLOTS)))
            r_parts.append(jnp.where(lane < 2 * SLOTS, lane_roll(one, 2 * SLOTS), two))
        c_row = jnp.concatenate(c_parts, axis=1)
        r_row = jnp.concatenate(r_parts, axis=1)
        at_col = (col_index == c_row).astype(f32).astype(bf16)
        arrived = got[pl.ds(g * PEERS, PEERS)].reshape(depth, width)
        turned = lax.dot_general(eye, arrived, nt, preferred_element_type=f32).astype(bf16)
        spread_ref[...] = turned

        @pl.loop(0, rows // 8)
        def _(q):
            stack = []
            for n in range(8):
                mask = (r_row == (q * 8 + n).astype(f32)).astype(f32).astype(bf16)
                stack.append(spread_ref[...] * mask)
            add = lax.dot_general(jnp.concatenate(stack, axis=0), at_col, nt, preferred_element_type=f32)
            for n in range(8):
                for half in range(2):
                    sum_ref[q * 8 + n, half] += add[n * width : (n + 1) * width, half * LANES : (half + 1) * LANES]

    @pl.loop(0, width)
    def _(n):
        out_ref[n] = adj_ref[n] + jnp.concatenate([sum_ref[:, 0, n, :], sum_ref[:, 1, n, :]], axis=1)

    @pl.loop(1, peers)
    def _(k):
        for copy in copies(k):
            copy.wait_send()


def exchange(adjoint, lidar, radiometer, counts):
    lat_count, lon_count = lax.axis_size("lat"), lax.axis_size("lon")
    peers = lat_count * lon_count
    bins, levels, rows, cols = adjoint.shape
    width = bins * levels
    obs_rows = lidar[0].shape[0]
    f32, bf16 = jnp.float32, jnp.bfloat16
    vmem = pl.BlockSpec(memory_space=pltpu.VMEM)
    smem = pl.BlockSpec(memory_space=pltpu.SMEM)
    out = pl.pallas_call(
        functools.partial(exchange_kernel, (2, lat_count // 2, 2, lon_count // 4)),
        out_shape=jax.ShapeDtypeStruct((width, rows, cols), f32),
        in_specs=[smem] + [vmem] * 9,
        out_specs=vmem,
        scratch_shapes=[
            pltpu.VMEM((2, obs_rows, 2 * width), bf16),
            pltpu.VMEM((2, 1, obs_rows), jnp.int32),
            pltpu.VMEM((PEERS * SLOTS, obs_rows), bf16),
            pltpu.VMEM((peers, 2 * SLOTS, width), bf16),
            pltpu.VMEM((peers, 2 * SLOTS, width), bf16),
            pltpu.VMEM((peers, 1, LANES), f32),
            pltpu.VMEM((peers, 1, LANES), f32),
            pltpu.VMEM((width, PEERS * 2 * SLOTS), bf16),
            pltpu.VMEM((rows, 2, width, LANES), f32),
            pltpu.SemaphoreType.DMA((peers,)),
            pltpu.SemaphoreType.DMA((peers,)),
            pltpu.SemaphoreType.DMA((peers,)),
            pltpu.SemaphoreType.DMA((peers,)),
        ],
        compiler_params=pltpu.CompilerParams(collective_id=1, has_side_effects=True, vmem_limit_bytes=60 << 20),
    )(
        counts,
        adjoint.reshape(width, rows, cols),
        lidar[0],
        radiometer[0],
        lidar[3],
        radiometer[3],
        lidar[1].reshape(1, obs_rows),
        radiometer[1].reshape(1, obs_rows),
        lidar[2].reshape(1, obs_rows),
        radiometer[2].reshape(1, obs_rows),
    )
    return out.reshape(adjoint.shape)


def per_device(
    adjoint_final,
    courant_lon,
    courant_lat,
    diffusivity,
    scavenging,
    lidar_innov,
    lidar_owner,
    lidar_column,
    radiometer_innov,
    radiometer_owner,
    radiometer_column,
    obs_count,
    lidar_op,
    radiometer_op,
):
    lidar = (lidar_innov, lidar_owner, lidar_column, lidar_op)
    radiometer = (radiometer_innov, radiometer_owner, radiometer_column, radiometer_op)
    adjoint = exchange(adjoint_final, lidar, radiometer, obs_count)
    return transport(adjoint, courant_lon, courant_lat, diffusivity, scavenging)


def solution(mesh):
    return jax.shard_map(
        per_device,
        mesh=mesh,
        in_specs=(
            P(None, None, "lat", "lon"),
            P(None, "lat", "lon"),
            P(None, "lat", "lon"),
            P(),
            P(),
            P(("lat", "lon"), None),
            P(("lat", "lon"), None),
            P(("lat", "lon")),
            P(("lat", "lon"), None),
            P(("lat", "lon"), None),
            P(("lat", "lon")),
            P(("lat", "lon"), None),
            P(),
            P(),
        ),
        out_specs=P(None, None, "lat", "lon"),
        check_vma=False,
    )
```

```python
import functools

import jax
import jax.numpy as jnp
from jax import lax
from jax.experimental import pallas as pl
from jax.experimental.pallas import tpu as pltpu
from jax.sharding import PartitionSpec as P

MESH = pl.DeviceIdType.MESH
STEPS = 3
LANES = 128
SLOTS = 32
PEERS = 8
BLOCK = 256
STACK = 8
PAD = 8


def lane_roll(x, amount):
    amount = amount % LANES
    return x if amount == 0 else pltpu.roll(x, amount, axis=1)


def wrapped(value, size):
    return jnp.where(value >= size, value - size, value)


def kernel(
    split,
    count_ref,
    diff_ref,
    lidar_ref,
    radio_ref,
    lidar_op_ref,
    radio_op_ref,
    lidar_owner_ref,
    radio_owner_ref,
    lidar_col_ref,
    radio_col_ref,
    adj_hbm,
    clon_hbm,
    clat_hbm,
    out_ref,
    table_ref,
    pos_ref,
    sent,
    got,
    sent_meta,
    got_meta,
    sum_ref,
    force_ref,
    adj_ref,
    clon_ref,
    clat_ref,
    c0_ref,
    ce_ref,
    cw_ref,
    cn_ref,
    cs_ref,
    even_ref,
    odd_ref,
    srow,
    rrow,
    scol,
    rcol,
    fsrow,
    frrow,
    fscol,
    frcol,
    send_sem,
    recv_sem,
    meta_send_sem,
    meta_recv_sem,
    row_send,
    row_recv,
    col_send,
    col_recv,
    face_send,
    face_recv,
    load_sem,
):
    f32, bf16 = jnp.float32, jnp.bfloat16
    lat_high, lat_low, lon_high, lon_low = split
    lat_count, lon_count = lat_high * lat_low, lon_high * lon_low * 2
    peers, _, width = sent.shape
    obs_rows = lidar_ref.shape[0]
    _, _, rows, _ = adj_ref.shape
    levels = clon_ref.shape[1]
    bins = width // levels
    lat = lax.axis_index("lat")
    lon = lax.axis_index("lon")
    yhigh, z = lax.div(lat, lat_low), lax.rem(lat, lat_low)
    core = lax.rem(lon, 2)
    x = lax.rem(lax.div(lon, 2), lon_low)
    ylow = lax.div(lon, 2 * lon_low)
    inner = [wrapped(x + p // 2, lon_low) * 2 + wrapped(core + p % 2, 2) for p in range(PEERS)]

    def group(g):
        to_ylow = wrapped(ylow + lax.rem(g, lon_high), lon_high)
        outer = lax.div(g, lon_high)
        to_z = wrapped(z + lax.rem(outer, lat_low), lat_low)
        to_yhigh = wrapped(yhigh + lax.div(outer, lat_low), lat_high)
        to_lat = to_yhigh * lat_low + to_z
        return [(to_lat, to_ylow * (2 * lon_low) + inner[p]) for p in range(PEERS)]

    def at(place):
        return {"lat": place[0], "lon": place[1]}

    barrier = pltpu.get_barrier_semaphore()

    def greet(place):
        pl.semaphore_signal(barrier, inc=1, device_id=at(place), device_id_type=MESH)

    for place in group(jnp.int32(0))[1:]:
        greet(place)

    @pl.loop(1, peers // PEERS)
    def _(g):
        for place in group(g):
            greet(place)

    def loads():
        pairs = []
        for half in range(2):
            lanes = pl.ds(half * LANES, LANES)
            pairs.append((clat_hbm.at[:, :, lanes], clat_ref.at[half, :, pl.ds(0, rows), :]))
            pairs.append((clon_hbm.at[:, :, lanes], clon_ref.at[half]))
            pairs.append((adj_hbm.at[:, :, lanes], adj_ref.at[half]))
        return [pltpu.make_async_copy(src, dst, load_sem.at[n]) for n, (src, dst) in enumerate(pairs)]

    for copy in loads():
        copy.start()

    earlier = (
        (lax.broadcasted_iota(jnp.int32, (BLOCK, BLOCK), 0) < lax.broadcasted_iota(jnp.int32, (BLOCK, BLOCK), 1))
        .astype(f32)
        .astype(bf16)
    )
    eye = (
        (lax.broadcasted_iota(jnp.int32, (16, width), 0) == lax.broadcasted_iota(jnp.int32, (16, width), 1))
        .astype(f32)
        .astype(bf16)
    )
    nt = (((1,), (1,)), ((), ()))
    cols = 2 * LANES

    def prepare(kind, values_ref, op_ref, owner_ref, col_ref):
        device = lax.broadcasted_iota(jnp.int32, (peers, BLOCK), 0)
        sub = lax.broadcasted_iota(jnp.int32, (width, BLOCK), 0)
        running = jnp.zeros((peers, 1), f32)
        for n in range(obs_rows // BLOCK):
            span = slice(n * BLOCK, (n + 1) * BLOCK)
            forces = jnp.dot(values_ref[span, :], op_ref[...], preferred_element_type=f32)
            table_ref[kind, span, 0:width] = forces.astype(bf16)
            column = col_ref[:, span]
            meta = jnp.where(sub == 0, column % cols, jnp.where(sub == 1, column // cols, 0)).astype(f32)
            table_ref[kind, span, width:] = meta.T.astype(bf16)
            index = n * BLOCK + lax.broadcasted_iota(jnp.int32, (1, BLOCK), 1)
            used = index < count_ref[0, kind]
            target = jnp.where(used, owner_ref[:, span], -1)
            member = (target == device).astype(f32)
            before = jnp.dot(member.astype(bf16), earlier, preferred_element_type=f32) + running
            slot = jnp.sum(before * member, axis=0, keepdims=True)
            running = running + jnp.sum(member, axis=1, keepdims=True)
            pos_ref[kind, :, span] = jnp.where(used, target * SLOTS + slot.astype(jnp.int32), -1)

    prepare(0, lidar_ref, lidar_op_ref, lidar_owner_ref, lidar_col_ref)
    prepare(1, radio_ref, radio_op_ref, radio_owner_ref, radio_col_ref)
    pl.semaphore_wait(barrier, peers - 1)

    def remote(src, dst, send, recv, there):
        return pltpu.make_async_remote_copy(
            src_ref=src, dst_ref=dst, send_sem=send, recv_sem=recv, device_id=there, device_id_type=MESH
        )

    def copies(k, place):
        return (
            remote(sent.at[k], got.at[k], send_sem.at[k], recv_sem.at[k], at(place)),
            remote(sent_meta.at[k], got_meta.at[k], meta_send_sem.at[k], meta_recv_sem.at[k], at(place)),
        )

    def own_copies():
        return (
            pltpu.make_async_copy(sent.at[0], got.at[0], recv_sem.at[0]),
            pltpu.make_async_copy(sent_meta.at[0], got_meta.at[0], meta_recv_sem.at[0]),
        )

    slot_index = lax.broadcasted_iota(jnp.int32, (SLOTS, obs_rows), 0)
    lane = lax.broadcasted_iota(jnp.int32, (1, LANES), 1)

    @pl.loop(0, peers // PEERS)
    def _(g):
        places = group(g)
        picks = []
        for kind in range(2):
            parts = []
            for p in range(PEERS):
                local = pos_ref[kind] - (places[p][0] * lon_count + places[p][1]) * SLOTS
                parts.append((slot_index == local).astype(f32).astype(bf16))
            picks.append(jnp.concatenate(parts, axis=0))
        both = [jnp.dot(picks[kind], table_ref[kind], preferred_element_type=f32).astype(bf16) for kind in range(2)]
        metas = []
        for kind in range(2):
            placed = both[kind]
            for p in range(PEERS):
                sent[g * PEERS + p, kind * SLOTS : (kind + 1) * SLOTS, :] = placed[p * SLOTS : (p + 1) * SLOTS, 0:width]
            metas.append(lax.dot_general(eye, placed[:, width:], nt, preferred_element_type=f32))
        for p in range(PEERS):

            def piece(kind, what, to):
                half = metas[kind][what : what + 1, p // 4 * LANES : (p // 4 + 1) * LANES]
                return lane_roll(half, to * SLOTS - p % 4 * SLOTS)

            low = jnp.where(lane < SLOTS, piece(0, 0, 0), piece(1, 0, 1))
            high = jnp.where(lane < 3 * SLOTS, piece(0, 1, 2), piece(1, 1, 3))
            sent_meta[g * PEERS + p] = jnp.where(lane < 2 * SLOTS, low, high)
        for p in range(1, PEERS):
            for copy in copies(g * PEERS + p, places[p]):
                copy.start()

        @pl.when(g > 0)
        def _():
            for copy in copies(g * PEERS, places[0]):
                copy.start()

        @pl.when(g == 0)
        def _():
            for copy in own_copies():
                copy.start()

    north = {"lat": wrapped(lat + 1, lat_count)}
    south = {"lat": wrapped(lat + lat_count - 1, lat_count)}
    east = {"lon": wrapped(lon + 1, lon_count)}
    west = {"lon": wrapped(lon + lon_count - 1, lon_count)}
    tall = clat_ref.shape[2]
    high = even_ref.shape[2]
    tile_lane = lax.broadcasted_iota(jnp.int32, (8, LANES), 1)
    is_first = tile_lane == 0
    is_last = tile_lane == LANES - 1

    def face_copies():
        return (
            remote(fsrow, frrow, face_send.at[0], face_recv.at[0], south),
            remote(fscol, frcol, face_send.at[1], face_recv.at[1], west),
        )

    for copy in loads():
        copy.wait()
    for half in range(2):
        fsrow[half] = clat_ref.at[half].reshape(levels * tall, LANES)[pl.ds(0, levels, stride=tall), :]
    for q in range(rows // 8):
        packed = jnp.zeros((8, LANES), f32)
        for l in range(levels):
            packed = jnp.where(tile_lane == l, lane_roll(clon_ref[0, l, 8 * q : 8 * q + 8, :], l), packed)
        fscol[8 * q : 8 * q + 8, :] = packed
    for copy in face_copies():
        copy.start()

    @pl.loop(0, rows)
    def _(r):
        sum_ref[r] = jnp.zeros((2, LANES, width), f32)

    depth = PEERS * 2 * SLOTS
    cell_index = lax.broadcasted_iota(jnp.int32, (LANES, depth), 0).astype(f32)

    @pl.loop(0, peers // PEERS)
    def _(g):
        places = group(g)
        for p in range(1, PEERS):
            for copy in copies(g * PEERS + p, places[p]):
                copy.wait_recv()

        @pl.when(g > 0)
        def _():
            for copy in copies(g * PEERS, places[0]):
                copy.wait_recv()

        @pl.when(g == 0)
        def _():
            for copy in own_copies():
                copy.wait()

        c_parts, r_parts = [], []
        for p in range(0, PEERS, 2):
            one, two = got_meta[g * PEERS + p], got_meta[g * PEERS + p + 1]
            c_parts.append(jnp.where(lane < 2 * SLOTS, one, lane_roll(two, 2 * SLOTS)))
            r_parts.append(jnp.where(lane < 2 * SLOTS, lane_roll(one, 2 * SLOTS), two))
        sides = []
        for n in range(PEERS // 2):
            right = jnp.broadcast_to((c_parts[n] >= LANES).astype(f32), (LANES, LANES)).T.astype(bf16)
            arrived = got[pl.ds(g * PEERS + 2 * n, 2)].reshape(4 * SLOTS, width)
            to_right = arrived * right
            sides.append(jnp.concatenate([arrived - to_right, to_right], axis=1))
        sides = jnp.concatenate(sides, axis=0)
        c_row = jnp.concatenate(c_parts, axis=1)
        r_row = jnp.concatenate(r_parts, axis=1)
        cell = r_row * LANES + jnp.where(c_row >= LANES, c_row - LANES, c_row)

        @pl.loop(0, rows // STACK)
        def _(q):
            start = (q * (STACK * LANES)).astype(f32)
            stack = [(cell_index == cell - (start + n * LANES)).astype(f32).astype(bf16) for n in range(STACK)]
            add = jnp.dot(jnp.concatenate(stack, axis=0), sides, preferred_element_type=f32)
            for n in range(STACK):
                for half in range(2):
                    sum_ref[q * STACK + n, half] += add[n * LANES : (n + 1) * LANES, half * width : (half + 1) * width]

    @pl.loop(0, rows)
    def _(r):
        for half in range(2):
            view = force_ref.at[half].reshape(width * rows, LANES)
            view[pl.ds(r, width, stride=rows), :] = sum_ref[r, half].T

    for copy in face_copies():
        copy.wait()
    for half in range(2):
        clat_ref.at[half].reshape(levels * tall, LANES)[pl.ds(rows, levels, stride=tall), :] = frrow[half]
    tile_row = lax.broadcasted_iota(jnp.int32, (8, LANES), 0)
    first_band = (lat == 0).astype(jnp.int32)
    last_band = (lat == lat_count - 1).astype(jnp.int32)
    south_open = jnp.where(tile_row + 8 * (1 - first_band) == 0, 0.0, 1.0)
    north_open = jnp.where(tile_row + 8 * (1 - last_band) == 7, 0.0, 1.0)

    @pl.loop(0, levels)
    def _(l):
        outer_shift = lax.rem(2 * LANES - 1 - l, LANES)
        for q in range(rows // 8):
            at8 = slice(8 * q, 8 * q + 8)
            faces = [clon_ref[half, l, at8, :] for half in range(2)]
            left, right = (lane_roll(face, LANES - 1) for face in faces)
            outer = pltpu.roll(frcol[at8, :], outer_shift, axis=1)
            beyond = [jnp.where(is_last, right, left), jnp.where(is_last, outer, right)]
            for half in range(2):
                lon_next = jnp.maximum(beyond[half], 0.0)
                lon_here = jnp.minimum(faces[half], 0.0)
                lat_next = jnp.maximum(clat_ref[half, l, 8 * q + 1 : 8 * q + 9, :], 0.0)
                lat_here = jnp.minimum(clat_ref[half, l, at8, :], 0.0)
                if q == 0:
                    lat_here = lat_here * south_open
                if q == rows // 8 - 1:
                    lat_next = lat_next * north_open
                ce_ref[half, l, at8, :] = lon_next
                cw_ref[half, l, at8, :] = lon_here
                cn_ref[half, l, at8, :] = lat_next
                cs_ref[half, l, at8, :] = lat_here
                c0_ref[half, l, at8, :] = 1.0 - lon_next + lon_here - lat_next + lat_here

    def halo_copies(t):
        return (
            remote(srow.at[0, t], rrow.at[0, t], row_send.at[0, t], row_recv.at[0, t], south),
            remote(srow.at[1, t], rrow.at[1, t], row_send.at[1, t], row_recv.at[1, t], north),
            remote(scol.at[0, t], rcol.at[0, t], col_send.at[0, t], col_recv.at[0, t], west),
            remote(scol.at[1, t], rcol.at[1, t], col_send.at[1, t], col_recv.at[1, t], east),
        )

    def mix_and_send(tile, dst, b, t):
        for q in range(rows // 8):
            at8 = slice(PAD + 8 * q, PAD + 8 * q + 8)
            packs = [jnp.zeros((8, LANES), f32)] * 2
            here = tile(q, 0)
            flux_low = None
            for l in range(levels):
                value = list(here)
                if l + 1 < levels:
                    above = tile(q, l + 1)
                    flux_high = [(above[half] - here[half]) * diff_ref[l] for half in range(2)]
                    value = [value[half] + flux_high[half] for half in range(2)]
                if flux_low is not None:
                    value = [value[half] - flux_low[half] for half in range(2)]
                for half in range(2):
                    dst[half, b * levels + l, at8, :] = value[half]
                packs = [
                    jnp.where(tile_lane == l, lane_roll(value[0], l), packs[0]),
                    jnp.where(tile_lane == l, lane_roll(value[1], l + 1), packs[1]),
                ]
                if l + 1 < levels:
                    here, flux_low = above, flux_high
            for side in range(2):
                scol[side, t, 8 * q : 8 * q + 8, :] = packs[side]
        for half in range(2):
            view = dst.at[half].reshape(width * high, LANES)
            srow[0, t, half] = view[pl.ds(b * (levels * high) + PAD, levels, stride=high), :]
            srow[1, t, half] = view[pl.ds(b * (levels * high) + PAD + rows - 1, levels, stride=high), :]
        for copy in halo_copies(t):
            copy.start()

    @pl.loop(0, bins)
    def _(b):
        def tile(q, l):
            at8 = slice(8 * q, 8 * q + 8)
            return [
                adj_ref[half, b * levels + l, at8, :] + force_ref[half, b * levels + l, at8, :] for half in range(2)
            ]

        mix_and_send(tile, even_ref, b, b)

    def arrive(src, b, t):
        for copy in halo_copies(t):
            copy.wait_recv()
        for half in range(2):
            view = src.at[half].reshape(width * high, LANES)
            view[pl.ds(b * (levels * high) + PAD + rows, levels, stride=high), :] = rrow[0, t, half]
            view[pl.ds(b * (levels * high) + PAD - 1, levels, stride=high), :] = rrow[1, t, half]

    def advected(src, b, t):
        def tile(q, l):
            at8 = slice(8 * q, 8 * q + 8)
            low = PAD + 8 * q
            m = [src[half, b * levels + l, low : low + 8, :] for half in range(2)]
            n = [src[half, b * levels + l, low + 1 : low + 9, :] for half in range(2)]
            s = [src[half, b * levels + l, low - 1 : low + 7, :] for half in range(2)]
            r = [lane_roll(v, 1) for v in m]
            f = [lane_roll(v, LANES - 1) for v in m]
            west_halo = lane_roll(rcol[1, t, at8, :], LANES - l)
            east_halo = lane_roll(rcol[0, t, at8, :], LANES - 1 - l)
            w = [jnp.where(is_first, west_halo, r[0]), jnp.where(is_first, r[0], r[1])]
            e = [jnp.where(is_last, f[1], f[0]), jnp.where(is_last, east_halo, f[1])]
            return [
                c0_ref[half, l, at8, :] * m[half]
                + ce_ref[half, l, at8, :] * e[half]
                - cw_ref[half, l, at8, :] * w[half]
                + cn_ref[half, l, at8, :] * n[half]
                - cs_ref[half, l, at8, :] * s[half]
                for half in range(2)
            ]

        return tile

    for step in range(1, STEPS):
        src, dst = (even_ref, odd_ref) if step % 2 else (odd_ref, even_ref)

        @pl.loop((step - 1) * bins, step * bins)
        def _(t):
            b = t - (step - 1) * bins
            arrive(src, b, t)
            mix_and_send(advected(src, b, t), dst, b, t + bins)

    src = (odd_ref, even_ref)[STEPS % 2]

    @pl.loop((STEPS - 1) * bins, STEPS * bins)
    def _(t):
        b = t - (STEPS - 1) * bins
        arrive(src, b, t)
        tile = advected(src, b, t)
        for q in range(rows // 8):
            for l in range(levels):
                value = tile(q, l)
                for half in range(2):
                    out_ref[b, l, 8 * q : 8 * q + 8, half * LANES : (half + 1) * LANES] = value[half]

    @pl.loop(0, STEPS * bins)
    def _(t):
        for copy in halo_copies(t):
            copy.wait_send()

    @pl.loop(0, peers // PEERS)
    def _(g):
        places = group(g)
        for p in range(1, PEERS):
            for copy in copies(g * PEERS + p, places[p]):
                copy.wait_send()

        @pl.when(g > 0)
        def _():
            for copy in copies(g * PEERS, places[0]):
                copy.wait_send()


def per_device(
    adjoint_final,
    courant_lon,
    courant_lat,
    diffusivity,
    scavenging,
    lidar_innov,
    lidar_owner,
    lidar_column,
    radiometer_innov,
    radiometer_owner,
    radiometer_column,
    obs_count,
    lidar_op,
    radiometer_op,
):
    lat_count, lon_count = lax.axis_size("lat"), lax.axis_size("lon")
    peers = lat_count * lon_count
    bins, levels, rows, cols = adjoint_final.shape
    width = bins * levels
    obs_rows = lidar_innov.shape[0]
    turns = STEPS * bins
    f32, bf16 = jnp.float32, jnp.bfloat16
    vmem = pl.BlockSpec(memory_space=pltpu.VMEM)
    smem = pl.BlockSpec(memory_space=pltpu.SMEM)
    hbm = pl.BlockSpec(memory_space=pl.ANY)
    coef = pltpu.VMEM((2, levels, rows, LANES), f32)
    padded = pltpu.VMEM((2, width, rows + 2 * PAD, LANES), f32)
    dma = pltpu.SemaphoreType.DMA
    out = pl.pallas_call(
        functools.partial(kernel, (2, lat_count // 2, 2, lon_count // 4)),
        out_shape=jax.ShapeDtypeStruct(adjoint_final.shape, f32),
        in_specs=[smem] * 2 + [vmem] * 8 + [hbm] * 3,
        out_specs=vmem,
        scratch_shapes=[
            pltpu.VMEM((2, obs_rows, 2 * width), bf16),
            pltpu.VMEM((2, 1, obs_rows), jnp.int32),
            pltpu.VMEM((peers, 2 * SLOTS, width), bf16),
            pltpu.VMEM((peers, 2 * SLOTS, width), bf16),
            pltpu.VMEM((peers, 1, LANES), f32),
            pltpu.VMEM((peers, 1, LANES), f32),
            pltpu.VMEM((rows, 2, LANES, width), f32),
            pltpu.VMEM((2, width, rows, LANES), f32),
            pltpu.VMEM((2, width, rows, LANES), f32),
            coef,
            pltpu.VMEM((2, levels, rows + 8, LANES), f32),
            coef,
            coef,
            coef,
            coef,
            coef,
            padded,
            padded,
            pltpu.VMEM((2, turns, 2, levels, LANES), f32),
            pltpu.VMEM((2, turns, 2, levels, LANES), f32),
            pltpu.VMEM((2, turns, rows, LANES), f32),
            pltpu.VMEM((2, turns, rows, LANES), f32),
            pltpu.VMEM((2, levels, LANES), f32),
            pltpu.VMEM((2, levels, LANES), f32),
            pltpu.VMEM((rows, LANES), f32),
            pltpu.VMEM((rows, LANES), f32),
            dma((peers,)),
            dma((peers,)),
            dma((peers,)),
            dma((peers,)),
            dma((2, turns)),
            dma((2, turns)),
            dma((2, turns)),
            dma((2, turns)),
            dma((2,)),
            dma((2,)),
            dma((6,)),
        ],
        compiler_params=pltpu.CompilerParams(collective_id=0, has_side_effects=True, vmem_limit_bytes=60 << 20),
    )(
        obs_count,
        diffusivity,
        lidar_innov,
        radiometer_innov,
        lidar_op,
        radiometer_op,
        lidar_owner.reshape(1, obs_rows),
        radiometer_owner.reshape(1, obs_rows),
        lidar_column.reshape(1, obs_rows),
        radiometer_column.reshape(1, obs_rows),
        adjoint_final.reshape(width, rows, cols),
        courant_lon,
        courant_lat,
    )
    return out * jnp.exp(-STEPS * scavenging)[:, None, None, None]


def solution(mesh):
    return jax.shard_map(
        per_device,
        mesh=mesh,
        in_specs=(
            P(None, None, "lat", "lon"),
            P(None, "lat", "lon"),
            P(None, "lat", "lon"),
            P(),
            P(),
            P(("lat", "lon"), None),
            P(("lat", "lon"), None),
            P(("lat", "lon")),
            P(("lat", "lon"), None),
            P(("lat", "lon"), None),
            P(("lat", "lon")),
            P(("lat", "lon"), None),
            P(),
            P(),
        ),
        out_specs=P(None, None, "lat", "lon"),
        check_vma=False,
    )
```
